32 devices in a mesh: amp: 4 (over y, core), own: 8 (over z, x).
Axes of the slice: x: 2, y: 2, z: 4, core: 2. Of those that a mesh axis runs over, the one named last changes fastest.
Arguments:
- amplitudes: bfloat16 [32, 2304, 192], P('own', None, 'amp'), may hold values from -6 to 6
- integrals: bfloat16 [32, 1152, 2304], P('own'), as said below
- occ_irrep: int32 [34], replicated, may hold values from 0 to 7, as said below
- tile_irrep: int32 [18], replicated, may hold values from 0 to 7, as said below
Outputs:
- cycle_term: bfloat16 [2304, 2304], P(('amp', 'own'))
The draws below stay inside these ranges and needn't reach their ends.
Inputs may be any that keep to these rules, and one draw needn't show every extreme that they name: `occ_irrep`: labels of the D2h group, combined by XOR; every label occurs, and all labels occur equally often up to one. `tile_irrep`: labels of the D2h group, combined by XOR; every label occurs, and all labels occur equally often up to one, so some label has exactly 3 tiles. integrals[k, c, (j, b)] is zero unless the labels of k, c, j and b combine by XOR to 0.
All inputs are finite; a program needn't handle non-finite values.
Results may differ from the reference program's by a relative error of at most 0.001.
Values may be sent and summed in bfloat16 or wider, within the bound.
A program may use at most 128 MiB of HBM per device.

```python
import jax
import jax.numpy as jnp
from jax import lax

V = 1152
TILE = 64
SLOTS = 3
NI = 2
NK = 32


def occ_labels(key):
    order = jax.random.permutation(jax.random.fold_in(key, 11), NI + NK)
    return (order % 8).astype(jnp.int32)


def tile_labels(key):
    order = jax.random.permutation(jax.random.fold_in(key, 23), V // TILE)
    return (order % 8).astype(jnp.int32)


def draw_occ_irrep(key, part):
    return occ_labels(key)


def draw_tile_irrep(key, part):
    return tile_labels(key)


def draw_integrals(key, part):
    occ = occ_labels(key)
    virt_lab = jnp.repeat(tile_labels(key), TILE)
    slab_lab = jnp.bitwise_xor(jnp.repeat(occ[:NI], V), jnp.tile(virt_lab, NI))
    k_lab = occ[NI:]
    values = jax.random.normal(jax.random.fold_in(key, 37), (NK, V, NI * V), jnp.float32)
    values = values * (NK * V / 8.0) ** (-0.5)
    labels = jnp.bitwise_xor(jnp.bitwise_xor(k_lab[:, None, None], virt_lab[None, :, None]), slab_lab[None, None, :])
    return jnp.where(labels == 0, values, jnp.zeros((), jnp.float32)).astype(jnp.bfloat16)


def raised(values, own_key, source, target, blocks, factor):
    def block_of(axis_at):
        return (jnp.arange(values.shape[axis_at]) // (values.shape[axis_at] // blocks)).reshape((-1,) + (1,) * (values.ndim - 1 - axis_at))

    near = jax.random.permutation(own_key, blocks)[block_of(target)]
    far = (block_of(target) + blocks // 2) % blocks
    return jnp.where((block_of(source) == near) | (block_of(source) == far), factor * values, values)


def level_of(key, dims, cuts, least, largest):
    def one(axis_at, parts):
        draws = jax.random.uniform(jax.random.fold_in(jax.random.fold_in(key, 6), axis_at), (parts,), jnp.float32, least / len(cuts), largest / len(cuts))
        return jnp.repeat(jnp.exp(draws), dims[axis_at] // parts).reshape((-1,) + (1,) * (len(dims) - axis_at - 1))

    factor_of = one(*cuts[0])
    for cut in cuts[1:]:
        factor_of = factor_of * one(*cut)
    return factor_of


def heavy_noise(own_key, shape, spread, most, cuts, heavy, kind=jnp.bfloat16):
    drawn = spread * jax.random.normal(own_key, shape, jnp.float32)
    if cuts:
        drawn = drawn * level_of(own_key, shape, cuts, -0.22, 0.18)
    return jnp.clip(raised(drawn, jax.random.fold_in(own_key, 3), *heavy), -most, most).astype(kind)


def setup_inputs(seed: int = 0) -> dict:
    key_of = jax.random.split(jax.random.key(seed), 5)
    return {
        "amplitudes": heavy_noise(key_of[0], (NK, NI * V, SLOTS * TILE), 1.0, 6.0, ((0, 8), (2, 4)), (0, 1, 8, 2.0)),
        "integrals": draw_integrals(jax.random.fold_in(key_of[4], 71), 0),
        "occ_irrep": draw_occ_irrep(jax.random.fold_in(key_of[4], 71), 0),
        "tile_irrep": draw_tile_irrep(jax.random.fold_in(key_of[4], 71), 0),
    }


def tile_ranks(tile_irrep):
    count = tile_irrep.shape[0]
    index = jnp.arange(count, dtype=jnp.int32)
    same = (tile_irrep[:, None] == tile_irrep[None, :]) & (index[None, :] < index[:, None])
    return jnp.sum(same.astype(jnp.int32), axis=1).astype(jnp.int32)


def unpack(packed, wanted, tile_irrep, ranks):
    slot_ids = jnp.arange(SLOTS, dtype=jnp.int32)
    select = (tile_irrep[None, None, :] == wanted[:, None, None]) & (ranks[None, None, :] == slot_ids[None, :, None])
    pieces = packed.astype(jnp.float32).reshape(packed.shape[0], SLOTS, TILE)
    dense = jnp.einsum("rjt,rje->rte", select.astype(jnp.float32), pieces)
    return dense.reshape(packed.shape[0], V).astype(jnp.bfloat16)


def reference(amplitudes, integrals, occ_irrep, tile_irrep):
    virt_lab = jnp.repeat(tile_irrep, TILE)
    row_lab = jnp.bitwise_xor(jnp.repeat(occ_irrep[:NI], V), jnp.tile(virt_lab, NI))
    k_labels = occ_irrep[NI:]
    ranks = tile_ranks(tile_irrep)

    def accumulate(total, items):
        block, weights, k_label = items
        dense = unpack(block, jnp.bitwise_xor(row_lab, k_label), tile_irrep, ranks)
        return total + jnp.dot(dense, weights, preferred_element_type=jnp.float32), None

    start = jnp.zeros((NI * V, NI * V), jnp.float32)
    cycle = lax.scan(accumulate, start, (amplitudes, integrals, k_labels))[0]
    return (cycle + cycle.T).astype(jnp.bfloat16)
```

```python
import functools

import jax
import jax.numpy as jnp
from jax import lax
from jax.experimental import pallas as pl
from jax.experimental.pallas import tpu as pltpu
from jax.sharding import PartitionSpec as P

TILE = 64
NI = 2
LABELS = 8
LANES = 128
MESH = pl.DeviceIdType.MESH


def gcd(a, b):
    return a if b == 0 else gcd(b, a % b)


def half_of(block, odd):
    return jnp.where(odd, block[:, TILE:], block[:, :TILE])


def local_kernel(n_tiles, slots, amp_ref, int_ref, occ_ref, tile_ref, out_ref, meta_ref, w_ref, tile_of, row_of, count, sems):
    k_local, rows, width = amp_ref.shape
    pieces, grain = w_ref.shape[1], w_ref.shape[2]
    wide = NI * slots
    amp_index = lax.axis_index("amp")
    own_index = lax.axis_index("own")

    for i in range(LABELS):
        count[i] = 0
        for s in range(slots):
            tile_of[i * slots + s] = -1
        for q in range(wide):
            row_of[i * wide + q] = -1
    for t in range(n_tiles):
        lab = tile_ref[t]
        rank = count[lab]
        tile_of[lab * slots + rank] = t
        count[lab] = rank + 1

    def copy_of(k, lab, j):
        at = amp_index * width + j * grain
        t = tile_of[lab * slots + at // TILE]
        start = pl.multiple_of(jnp.maximum(t, 0) * TILE + at % TILE, grain)
        copy = pltpu.make_async_copy(
            int_ref.at[k, pl.ds(start, grain), :], w_ref.at[k * LABELS + lab, j], sems.at[k, lab, j]
        )
        return t, copy

    for k in range(k_local):
        for lab in range(LABELS):
            for j in range(pieces):
                t, copy = copy_of(k, lab, j)

                @pl.when(t >= 0)
                def _():
                    copy.start()

                @pl.when(t < 0)
                def _():
                    w_ref[k * LABELS + lab, j] = jnp.zeros((grain, rows), w_ref.dtype)

    for i in range(LABELS):
        count[i] = 0
    for u in range(NI * n_tiles):
        lab = jnp.bitwise_xor(occ_ref[u // n_tiles], tile_ref[u % n_tiles])
        rank = count[lab]
        row_of[lab * wide + rank] = u
        count[lab] = rank + 1
        meta_ref[u] = lab
        meta_ref[NI * n_tiles + u] = rank

    k_lab = [occ_ref[NI + own_index * k_local + k] for k in range(k_local)]

    for k in range(k_local):
        for lab in range(LABELS):
            for j in range(pieces):
                t, copy = copy_of(k, lab, j)

                @pl.when(t >= 0)
                def _():
                    copy.wait()

    def block(lab, carry):
        tiles = [jnp.maximum(row_of[lab * wide + q], 0) for q in range(wide)]
        a = jnp.concatenate(
            [
                jnp.concatenate(
                    [amp_ref[k, pl.ds(pl.multiple_of(u * TILE, TILE), TILE), :] for k in range(k_local)], axis=1
                )
                for u in tiles
            ],
            axis=0,
        )
        stack = []
        for k in range(k_local):
            at = k * LABELS + jnp.bitwise_xor(lab, k_lab[k])
            halves = []
            for u in tiles:
                lanes = pl.ds(pl.multiple_of(u // 2 * LANES, LANES), LANES)
                x = w_ref[at, :, :, lanes].reshape(pieces * grain, LANES)
                halves.append(half_of(x, u % 2 == 1))
            stack.append(jnp.concatenate(halves, axis=1))
        w = jnp.concatenate(stack, axis=0)
        p = jnp.dot(a, w, preferred_element_type=jnp.float32)
        s = p + p.T
        for q in range(wide):
            u = row_of[lab * wide + q]

            @pl.when(u >= 0)
            def _():
                for c in range(out_ref.shape[0]):
                    out_ref[c, pl.ds(pl.multiple_of(u * TILE, TILE), TILE), :] = s[
                        q * TILE : (q + 1) * TILE, c * LANES : (c + 1) * LANES
                    ]

        return carry

    lax.fori_loop(0, LABELS, block, 0)


def orders(amp_bits, own_bits):
    core = [("amp", 0)]
    y = [("amp", b) for b in range(1, amp_bits)]
    near = [("own", 0)]
    far = [("own", b) for b in range(1, own_bits)]
    return [core + y + near + far, core + near + y + far, core + far + y + near]


def bit_of(name, bit):
    return lax.axis_index(name) // 2**bit % 2


def partner_of(name, bit):
    return {name: lax.axis_index(name) + (1 - 2 * bit_of(name, bit)) * 2**bit}


def scatter_kernel(plans, x_ref, out_ref, *scratch):
    stages = len(plans[0])
    accs = [[scratch[(c * stages + s) * 2] for s in range(stages)] for c in range(len(plans))]
    recvs = [[scratch[(c * stages + s) * 2 + 1] for s in range(stages)] for c in range(len(plans))]
    send_sems, recv_sems = scratch[-2:]

    barrier = pltpu.get_barrier_semaphore()
    for name, bit, _ in plans[0]:
        pl.semaphore_signal(barrier, inc=1, device_id=partner_of(name, bit), device_id_type=MESH)
    pl.semaphore_wait(barrier, stages)

    def copy_of(c, s):
        name, bit, axis = plans[c][s]
        held = x_ref.at[c] if s == 0 else accs[c][s - 1]
        return pltpu.make_async_remote_copy(
            src_ref=held.at[(slice(None),) * axis + (1 - bit_of(name, bit),)],
            dst_ref=recvs[c][s],
            send_sem=send_sems.at[c, s],
            recv_sem=recv_sems.at[c, s],
            device_id=partner_of(name, bit),
            device_id_type=MESH,
        )

    for c in range(len(plans)):
        copy_of(c, 0).start()
    for s in range(stages):
        for c in range(len(plans)):
            name, bit, axis = plans[c][s]
            copy_of(c, s).wait_recv()
            held = x_ref.at[c] if s == 0 else accs[c][s - 1]
            index = (slice(None),) * axis + (bit_of(name, bit),)
            total = held[index] + recvs[c][s][...]
            if s + 1 < stages:
                accs[c][s][...] = total
                copy_of(c, s + 1).start()
            else:
                out_ref[c] = total
    for s in range(stages):
        for c in range(len(plans)):
            copy_of(c, s).wait_send()


def expand_kernel(n_tiles, x_ref, meta_ref, out_ref):
    chunks, share, _ = x_ref.shape
    count = NI * n_tiles
    base = (lax.axis_index("amp") * lax.axis_size("own") + lax.axis_index("own")) * share
    first = base // TILE
    row = base + lax.broadcasted_iota(jnp.int32, (share, LANES), 0)
    lane = lax.broadcasted_iota(jnp.int32, (share, LANES), 1)
    row_lab = jnp.where(row < (first + 1) * TILE, meta_ref[first], meta_ref[jnp.minimum(first + 1, count - 1)])
    for pair in range(count // 2):
        labs = [meta_ref[2 * pair + h] for h in range(2)]
        ranks = [meta_ref[count + 2 * pair + h] for h in range(2)]
        halves = [half_of(x_ref[rank // 2], rank % 2 == 1) for rank in ranks]
        col_lab = jnp.where(lane < TILE, labs[0], labs[1])
        dense = jnp.where(row_lab == col_lab, jnp.concatenate(halves, axis=1), 0.0)
        out_ref[:, pair * LANES : (pair + 1) * LANES] = dense.astype(out_ref.dtype)


def shards(amplitudes, integrals, occ_irrep, tile_irrep):
    n_amp = lax.axis_size("amp")
    n_own = lax.axis_size("own")
    k_local, rows, width = amplitudes.shape
    n_tiles = tile_irrep.shape[0]
    slots = width * n_amp // TILE
    grain = gcd(width, TILE)
    chunks = NI * slots * TILE // LANES
    vmem, smem, hbm = (pl.BlockSpec(memory_space=m) for m in (pltpu.VMEM, pltpu.SMEM, pl.ANY))
    packed, meta = pl.pallas_call(
        functools.partial(local_kernel, n_tiles, slots),
        out_shape=(
            jax.ShapeDtypeStruct((chunks, rows, LANES), jnp.float32),
            jax.ShapeDtypeStruct((2 * NI * n_tiles,), jnp.int32),
        ),
        in_specs=[vmem, hbm, smem, smem],
        out_specs=(vmem, smem),
        scratch_shapes=[
            pltpu.VMEM((k_local * LABELS, width // grain, grain, rows), jnp.bfloat16),
            pltpu.SMEM((LABELS * slots,), jnp.int32),
            pltpu.SMEM((LABELS * NI * slots,), jnp.int32),
            pltpu.SMEM((LABELS,), jnp.int32),
            pltpu.SemaphoreType.DMA((k_local, LABELS, width // grain)),
        ],
        compiler_params=pltpu.CompilerParams(vmem_limit_bytes=40 * 2**20),
        name="local",
    )(amplitudes, integrals, occ_irrep, tile_irrep)

    amp_bits, own_bits = n_amp.bit_length() - 1, n_own.bit_length() - 1
    share = rows // (n_amp * n_own)
    plans, scratch = [], []
    for order in orders(amp_bits, own_bits):
        left = [("amp", b) for b in reversed(range(amp_bits))] + [("own", b) for b in reversed(range(own_bits))]
        plan = []
        for name, bit in order:
            axis = left.index((name, bit))
            left.pop(axis)
            plan.append((name, bit, axis))
            scratch += [pltpu.VMEM((2,) * len(left) + (share, LANES), jnp.float32)] * 2
        plans.append(plan)
    stages = amp_bits + own_bits
    summed = pl.pallas_call(
        functools.partial(scatter_kernel, plans),
        out_shape=jax.ShapeDtypeStruct((chunks, share, LANES), jnp.float32),
        in_specs=[vmem],
        out_specs=vmem,
        scratch_shapes=scratch
        + [pltpu.SemaphoreType.DMA((chunks, stages)), pltpu.SemaphoreType.DMA((chunks, stages))],
        compiler_params=pltpu.CompilerParams(
            collective_id=0, has_side_effects=True, vmem_limit_bytes=40 * 2**20
        ),
        name="scatter",
    )(packed.reshape((chunks,) + (2,) * stages + (share, LANES)))

    return pl.pallas_call(
        functools.partial(expand_kernel, n_tiles),
        out_shape=jax.ShapeDtypeStruct((share, rows), jnp.bfloat16),
        in_specs=[vmem, smem],
        out_specs=vmem,
        name="expand",
    )(summed, meta)


def solution(mesh):
    return jax.shard_map(
        shards,
        mesh=mesh,
        in_specs=(P("own", None, "amp"), P("own", None, None), P(), P()),
        out_specs=P(("amp", "own"), None),
        check_vma=False,
    )
```

```python
import functools
import itertools

import jax
import jax.numpy as jnp
from jax import lax
from jax.experimental import pallas as pl
from jax.experimental.pallas import tpu as pltpu
from jax.sharding import PartitionSpec as P

TILE = 64
NI = 2
LABELS = 8
LANES = 128
LEVELS = 32767.0
LEAST = 1e-30
MESH = pl.DeviceIdType.MESH


def gcd(a, b):
    return a if b == 0 else gcd(b, a % b)


def half_of(block, odd):
    return jnp.where(odd, block[:, TILE:], block[:, :TILE])


def local_kernel(n_tiles, slots, amp_hbm, int_ref, occ_ref, tile_ref, out_ref, meta_ref, amp_ref, w_ref, tile_of, row_of, count, amp_sem, sems):
    k_local, rows, width = amp_hbm.shape
    pieces, grain = w_ref.shape[2], w_ref.shape[3]
    wide = NI * slots
    amp_index = lax.axis_index("amp")
    own_index = lax.axis_index("own")

    for i in range(LABELS):
        count[i] = 0
        for s in range(slots):
            tile_of[i * slots + s] = -1
        for q in range(wide):
            row_of[i * wide + q] = -1
    for t in range(n_tiles):
        lab = tile_ref[t]
        rank = count[lab]
        tile_of[lab * slots + rank] = t
        count[lab] = rank + 1

    amp_copy = pltpu.make_async_copy(amp_hbm, amp_ref, amp_sem)
    amp_copy.start()

    def copy_of(lab, j):
        at = amp_index * width + j * grain
        t = tile_of[lab * slots + at // TILE]
        start = pl.multiple_of(jnp.maximum(t, 0) * TILE + at % TILE, grain)
        copy = pltpu.make_async_copy(int_ref.at[:, pl.ds(start, grain), :], w_ref.at[lab, :, j], sems.at[lab, j])
        return t, copy

    for lab in range(LABELS):
        for j in range(pieces):
            t, copy = copy_of(lab, j)

            @pl.when(t >= 0)
            def _():
                copy.start()

            @pl.when(t < 0)
            def _():
                w_ref[lab, :, j] = jnp.zeros((k_local, grain, rows), w_ref.dtype)

    for i in range(LABELS):
        count[i] = 0
    for u in range(NI * n_tiles):
        lab = jnp.bitwise_xor(occ_ref[u // n_tiles], tile_ref[u % n_tiles])
        rank = count[lab]
        row_of[lab * wide + rank] = u
        count[lab] = rank + 1
        meta_ref[u] = lab
        meta_ref[NI * n_tiles + u] = rank

    k_lab = [occ_ref[NI + own_index * k_local + k] for k in range(k_local)]

    amp_copy.wait()
    for lab in range(LABELS):
        for j in range(pieces):
            t, copy = copy_of(lab, j)

            @pl.when(t >= 0)
            def _():
                copy.wait()

    def block(lab, carry):
        tiles = [jnp.maximum(row_of[lab * wide + q], 0) for q in range(wide)]
        a = jnp.concatenate(
            [
                jnp.concatenate(
                    [amp_ref[k, pl.ds(pl.multiple_of(u * TILE, TILE), TILE), :] for k in range(k_local)], axis=1
                )
                for u in tiles
            ],
            axis=0,
        )
        stack = []
        for k in range(k_local):
            at = jnp.bitwise_xor(lab, k_lab[k])
            halves = []
            for u in tiles:
                lanes = pl.ds(pl.multiple_of(u // 2 * LANES, LANES), LANES)
                x = w_ref[at, k, :, :, lanes].reshape(pieces * grain, LANES)
                halves.append(half_of(x, u % 2 == 1))
            stack.append(jnp.concatenate(halves, axis=1))
        w = jnp.concatenate(stack, axis=0)
        s = jnp.dot(a, w, preferred_element_type=jnp.float32) + lax.dot_general(
            w, a, (((0,), (1,)), ((), ())), preferred_element_type=jnp.float32
        )
        for q in range(wide):
            u = row_of[lab * wide + q]

            @pl.when(u >= 0)
            def _():
                for c in range(out_ref.shape[0]):
                    out_ref[c, pl.ds(pl.multiple_of(u * TILE, TILE), TILE), :] = s[
                        q * TILE : (q + 1) * TILE, c * LANES : (c + 1) * LANES
                    ]

        return carry

    lax.fori_loop(0, LABELS, block, 0)


def orders(amp_bits, own_bits):
    core = [("amp", 0)]
    y = [("amp", b) for b in range(1, amp_bits)]
    near = [("own", 0)]
    far = [("own", b) for b in range(1, own_bits)]
    return [core + y + near + far, core + near + y + far, core + far + y + near]


def bit_of(name, bit):
    return lax.axis_index(name) // 2**bit % 2


def partner_of(name, bit):
    return {name: lax.axis_index(name) + (1 - 2 * bit_of(name, bit)) * 2**bit}


def scatter_kernel(plans, x_ref, out_ref, *scratch):
    stages = len(plans[0])
    bufs, at = [], 0
    for c in range(len(plans)):
        bufs.append([])
        for s in range(stages):
            take = 2 if s == 0 else 5
            bufs[c].append(scratch[at : at + take])
            at += take
    send_sems, recv_sems, scale_send_sems, scale_recv_sems = scratch[at:]

    barrier = pltpu.get_barrier_semaphore()
    for name, bit, _ in plans[0]:
        pl.semaphore_signal(barrier, inc=1, device_id=partner_of(name, bit), device_id_type=MESH)
    pl.semaphore_wait(barrier, stages)

    def remote(c, s, src, dst, send, recv):
        name, bit, _ = plans[c][s]
        return pltpu.make_async_remote_copy(
            src_ref=src,
            dst_ref=dst,
            send_sem=send.at[c, s],
            recv_sem=recv.at[c, s],
            device_id=partner_of(name, bit),
            device_id_type=MESH,
        )

    def copies_of(c, s):
        name, bit, axis = plans[c][s]
        if s == 0:
            src = x_ref.at[(c,) + (slice(None),) * axis + (1 - bit_of(name, bit),)]
            return [remote(c, s, src, bufs[c][s][1], send_sems, recv_sems)]
        _, q_send, q_recv, scale_send, scale_recv = bufs[c][s]
        return [
            remote(c, s, scale_send, scale_recv, scale_send_sems, scale_recv_sems),
            remote(c, s, q_send, q_recv, send_sems, recv_sems),
        ]

    def blocks(count):
        return itertools.product(range(2), repeat=count)

    def quantize(c, s):
        name, bit, axis = plans[c][s]
        _, q_send, _, scale_send, _ = bufs[c][s]
        away = 1 - bit_of(name, bit)
        for index in blocks(stages - 1 - s):
            x = bufs[c][s - 1][0][index[:axis] + (away,) + index[axis:]]
            most = jnp.maximum(jnp.max(jnp.abs(x), axis=0, keepdims=True), LEAST)
            q_send[index] = jnp.round(x * (LEVELS / most)).astype(jnp.int32).astype(jnp.int16)
            scale_send[index] = most * (1.0 / LEVELS)

    for c in range(len(plans)):
        for copy in copies_of(c, 0):
            copy.start()
    for s in range(stages):
        for c in range(len(plans)):
            name, bit, axis = plans[c][s]
            keep = bit_of(name, bit)
            for copy in copies_of(c, s):
                copy.wait_recv()
            for index in blocks(stages - 1 - s):
                kept = index[:axis] + (keep,) + index[axis:]
                if s == 0:
                    total = x_ref[(c,) + kept] + bufs[c][s][1][index]
                else:
                    _, _, q_recv, _, scale_recv = bufs[c][s]
                    total = bufs[c][s - 1][0][kept] + q_recv[index].astype(jnp.int32).astype(jnp.float32) * scale_recv[index]
                if s + 1 < stages:
                    bufs[c][s][0][index] = total
                else:
                    out_ref[c] = total
            if s + 1 < stages:
                quantize(c, s + 1)
                for copy in copies_of(c, s + 1):
                    copy.start()
    for s in range(stages):
        for c in range(len(plans)):
            for copy in copies_of(c, s):
                copy.wait_send()


def expand_kernel(n_tiles, x_ref, meta_ref, out_ref):
    chunks, share, _ = x_ref.shape
    count = NI * n_tiles
    base = (lax.axis_index("amp") * lax.axis_size("own") + lax.axis_index("own")) * share
    first = base // TILE
    row = base + lax.broadcasted_iota(jnp.int32, (share, LANES), 0)
    lane = lax.broadcasted_iota(jnp.int32, (share, LANES), 1)
    row_lab = jnp.where(row < (first + 1) * TILE, meta_ref[first], meta_ref[jnp.minimum(first + 1, count - 1)])
    for pair in range(count // 2):
        labs = [meta_ref[2 * pair + h] for h in range(2)]
        ranks = [meta_ref[count + 2 * pair + h] for h in range(2)]
        halves = [half_of(x_ref[rank // 2], rank % 2 == 1) for rank in ranks]
        col_lab = jnp.where(lane < TILE, labs[0], labs[1])
        dense = jnp.where(row_lab == col_lab, jnp.concatenate(halves, axis=1), 0.0)
        out_ref[:, pair * LANES : (pair + 1) * LANES] = dense.astype(out_ref.dtype)


def shards(amplitudes, integrals, occ_irrep, tile_irrep):
    n_amp = lax.axis_size("amp")
    n_own = lax.axis_size("own")
    k_local, rows, width = amplitudes.shape
    n_tiles = tile_irrep.shape[0]
    slots = width * n_amp // TILE
    grain = gcd(width, TILE)
    chunks = NI * slots * TILE // LANES
    vmem, smem, hbm = (pl.BlockSpec(memory_space=m) for m in (pltpu.VMEM, pltpu.SMEM, pl.ANY))
    packed, meta = pl.pallas_call(
        functools.partial(local_kernel, n_tiles, slots),
        out_shape=(
            jax.ShapeDtypeStruct((chunks, rows, LANES), jnp.float32),
            jax.ShapeDtypeStruct((2 * NI * n_tiles,), jnp.int32),
        ),
        in_specs=[hbm, hbm, smem, smem],
        out_specs=(vmem, smem),
        scratch_shapes=[
            pltpu.VMEM((k_local, rows, width), jnp.bfloat16),
            pltpu.VMEM((LABELS, k_local, width // grain, grain, rows), jnp.bfloat16),
            pltpu.SMEM((LABELS * slots,), jnp.int32),
            pltpu.SMEM((LABELS * NI * slots,), jnp.int32),
            pltpu.SMEM((LABELS,), jnp.int32),
            pltpu.SemaphoreType.DMA,
            pltpu.SemaphoreType.DMA((LABELS, width // grain)),
        ],
        compiler_params=pltpu.CompilerParams(vmem_limit_bytes=40 * 2**20),
        name="local",
    )(amplitudes, integrals, occ_irrep, tile_irrep)

    amp_bits, own_bits = n_amp.bit_length() - 1, n_own.bit_length() - 1
    share = rows // (n_amp * n_own)
    plans, scratch = [], []
    for order in orders(amp_bits, own_bits):
        left = [("amp", b) for b in reversed(range(amp_bits))] + [("own", b) for b in reversed(range(own_bits))]
        plan = []
        for name, bit in order:
            axis = left.index((name, bit))
            left.pop(axis)
            plan.append((name, bit, axis))
            lead = (2,) * len(left)
            whole = pltpu.VMEM(lead + (share, LANES), jnp.float32)
            coded = pltpu.VMEM(lead + (share, LANES), jnp.int16)
            scale = pltpu.VMEM(lead + (1, LANES), jnp.float32)
            scratch += [whole, whole] if not plan[1:] else [whole, coded, coded, scale, scale]
        plans.append(plan)
    stages = amp_bits + own_bits
    summed = pl.pallas_call(
        functools.partial(scatter_kernel, plans),
        out_shape=jax.ShapeDtypeStruct((chunks, share, LANES), jnp.float32),
        in_specs=[vmem],
        out_specs=vmem,
        scratch_shapes=scratch
        + [pltpu.SemaphoreType.DMA((chunks, stages))] * 4,
        compiler_params=pltpu.CompilerParams(
            collective_id=0, has_side_effects=True, vmem_limit_bytes=40 * 2**20
        ),
        name="scatter",
    )(packed.reshape((chunks,) + (2,) * stages + (share, LANES)))

    return pl.pallas_call(
        functools.partial(expand_kernel, n_tiles),
        out_shape=jax.ShapeDtypeStruct((share, rows), jnp.bfloat16),
        in_specs=[vmem, smem],
        out_specs=vmem,
        name="expand",
    )(summed, meta)


def solution(mesh):
    return jax.shard_map(
        shards,
        mesh=mesh,
        in_specs=(P("own", None, "amp"), P("own", None, None), P(), P()),
        out_specs=P(("amp", "own"), None),
        check_vma=False,
    )
```

```python
import functools
import itertools

import jax
import jax.numpy as jnp
from jax import lax
from jax.experimental import pallas as pl
from jax.experimental.pallas import tpu as pltpu
from jax.sharding import PartitionSpec as P

TILE = 64
NI = 2
LABELS = 8
LANES = 128
LEVELS = 32767.0
LEAST = 1e-30
MESH = pl.DeviceIdType.MESH


def gcd(a, b):
    return a if b == 0 else gcd(b, a % b)


def local_kernel(n_tiles, slots, amp_hbm, int_ref, occ_hbm, tile_hbm, out_ref, amp_ref, w_ref, occ_ref, tile_ref, tile_of, row_of, count, local_sems, sems):
    k_local, width, rows = amp_hbm.shape
    pieces, grain = w_ref.shape[2], w_ref.shape[3]
    wide = NI * slots
    amp_index = lax.axis_index("amp")
    own_index = lax.axis_index("own")

    amp_copy = pltpu.make_async_copy(amp_hbm, amp_ref, local_sems.at[0])
    occ_copy = pltpu.make_async_copy(occ_hbm, occ_ref, local_sems.at[1])
    tile_copy = pltpu.make_async_copy(tile_hbm, tile_ref, local_sems.at[2])
    tile_copy.start()
    occ_copy.start()
    amp_copy.start()

    for i in range(LABELS):
        count[i] = 0
        for s in range(slots):
            tile_of[i * slots + s] = -1
        for q in range(wide):
            row_of[i * wide + q] = -1
    tile_copy.wait()
    for t in range(n_tiles):
        lab = tile_ref[t]
        rank = count[lab]
        tile_of[lab * slots + rank] = t
        count[lab] = rank + 1

    def copy_of(lab, j):
        at = amp_index * width + j * grain
        t = tile_of[lab * slots + at // TILE]
        start = pl.multiple_of(jnp.maximum(t, 0) * TILE + at % TILE, grain)
        copy = pltpu.make_async_copy(int_ref.at[:, pl.ds(start, grain), :], w_ref.at[lab, :, j], sems.at[lab, j])
        return t, copy

    for lab in range(LABELS):
        for j in range(pieces):
            t, copy = copy_of(lab, j)

            @pl.when(t >= 0)
            def _():
                copy.start()

            @pl.when(t < 0)
            def _():
                w_ref[lab, :, j] = jnp.zeros((k_local, grain, rows), w_ref.dtype)

    for i in range(LABELS):
        count[i] = 0
    occ_copy.wait()
    for u in range(NI * n_tiles):
        lab = jnp.bitwise_xor(occ_ref[u // n_tiles], tile_ref[u % n_tiles])
        rank = count[lab]
        row_of[lab * wide + rank] = u
        count[lab] = rank + 1

    k_lab = [occ_ref[NI + own_index * k_local + k] for k in range(k_local)]

    amp_copy.wait()
    for lab in range(LABELS):
        for j in range(pieces):
            t, copy = copy_of(lab, j)

            @pl.when(t >= 0)
            def _():
                copy.wait()

    low = lax.broadcasted_iota(jnp.int32, (width, LANES), 1) < TILE

    def block(lab, carry):
        tiles = [jnp.maximum(row_of[lab * wide + q], 0) for q in range(wide)]
        lanes = [pl.ds(pl.multiple_of(u // 2 * LANES, LANES), LANES) for u in tiles]

        def gather(load):
            turned = [pltpu.roll(load(at), (u + q) % 2 * TILE, 1) for q, (at, u) in enumerate(zip(lanes, tiles))]
            return jnp.concatenate([jnp.where(low, *turned[q : q + 2]) for q in range(0, wide, 2)], axis=1)

        a = [gather(lambda at: amp_ref[k, :, at]) for k in range(k_local)]
        w = [
            gather(lambda at: w_ref[jnp.bitwise_xor(lab, k_lab[k]), k, :, :, at].reshape(width, LANES))
            for k in range(k_local)
        ]
        s = lax.dot_general(
            jnp.concatenate(a + w, axis=0),
            jnp.concatenate(w + a, axis=0),
            (((0,), (0,)), ((), ())),
            preferred_element_type=jnp.float32,
        )
        for q in range(wide):
            u = row_of[lab * wide + q]

            @pl.when(u >= 0)
            def _():
                for c in range(out_ref.shape[0]):
                    out_ref[c, pl.ds(pl.multiple_of(u * TILE, TILE), TILE), :] = s[
                        q * TILE : (q + 1) * TILE, c * LANES : (c + 1) * LANES
                    ]

        return carry

    lax.fori_loop(0, LABELS, block, 0)


def orders(amp_bits, own_bits):
    core = [("amp", 0)]
    y = [("amp", b) for b in range(1, amp_bits)]
    near = [("own", 0)]
    far = [("own", b) for b in range(1, own_bits)]
    return [core + y + near + far, core + near + y + far, core + far + y + near]


def bit_of(name, bit):
    return lax.axis_index(name) // 2**bit % 2


def partner_of(name, bit):
    return {name: lax.axis_index(name) + (1 - 2 * bit_of(name, bit)) * 2**bit}


def scatter_kernel(plans, x_ref, occ_ref, tile_ref, out_ref, *scratch):
    stages = len(plans[0])
    bufs, at = [], 0
    for c in range(len(plans)):
        bufs.append([])
        for s in range(stages):
            take = 2 if s == 0 else 5
            bufs[c].append(scratch[at : at + take])
            at += take
    fin_ref, lab_ref, rank_ref, send_sems, recv_sems, scale_send_sems, scale_recv_sems = scratch[at:]

    barrier = pltpu.get_barrier_semaphore()
    for name, bit, _ in plans[0]:
        pl.semaphore_signal(barrier, inc=1, device_id=partner_of(name, bit), device_id_type=MESH)
    pl.semaphore_wait(barrier, stages)

    def remote(c, s, src, dst, send, recv):
        name, bit, _ = plans[c][s]
        return pltpu.make_async_remote_copy(
            src_ref=src,
            dst_ref=dst,
            send_sem=send.at[c, s],
            recv_sem=recv.at[c, s],
            device_id=partner_of(name, bit),
            device_id_type=MESH,
        )

    def copies_of(c, s):
        name, bit, axis = plans[c][s]
        if s == 0:
            src = x_ref.at[(c,) + (slice(None),) * axis + (1 - bit_of(name, bit),)]
            return [remote(c, s, src, bufs[c][s][1], send_sems, recv_sems)]
        _, q_send, q_recv, scale_send, scale_recv = bufs[c][s]
        return [
            remote(c, s, scale_send, scale_recv, scale_send_sems, scale_recv_sems),
            remote(c, s, q_send, q_recv, send_sems, recv_sems),
        ]

    def blocks(count):
        return itertools.product(range(2), repeat=count)

    def quantize(c, s):
        name, bit, axis = plans[c][s]
        _, q_send, _, scale_send, _ = bufs[c][s]
        away = 1 - bit_of(name, bit)
        for index in blocks(stages - 1 - s):
            x = bufs[c][s - 1][0][index[:axis] + (away,) + index[axis:]]
            most = jnp.maximum(jnp.max(jnp.abs(x), axis=0, keepdims=True), LEAST)
            q_send[index] = jnp.round(x * (LEVELS / most)).astype(jnp.int32).astype(jnp.int16)
            scale_send[index] = most * (1.0 / LEVELS)

    for c in range(len(plans)):
        for copy in copies_of(c, 0):
            copy.start()
    n_tiles = tile_ref.shape[0]
    labs = [jnp.bitwise_xor(occ_ref[u // n_tiles], tile_ref[u % n_tiles]) for u in range(NI * n_tiles)]
    for u, lab in enumerate(labs):
        lab_ref[u] = lab
        rank = jnp.int32(0)
        for other in labs[:u]:
            rank = rank + jnp.where(other == lab, 1, 0)
        rank_ref[u] = rank
    for s in range(stages):
        for c in range(len(plans)):
            name, bit, axis = plans[c][s]
            keep = bit_of(name, bit)
            for copy in copies_of(c, s):
                copy.wait_recv()
            for index in blocks(stages - 1 - s):
                kept = index[:axis] + (keep,) + index[axis:]
                if s == 0:
                    total = x_ref[(c,) + kept] + bufs[c][s][1][index]
                else:
                    _, _, q_recv, _, scale_recv = bufs[c][s]
                    total = bufs[c][s - 1][0][kept] + q_recv[index].astype(jnp.int32).astype(jnp.float32) * scale_recv[index]
                if s + 1 < stages:
                    bufs[c][s][0][index] = total
                else:
                    fin_ref[c] = total
            if s + 1 < stages:
                quantize(c, s + 1)
                for copy in copies_of(c, s + 1):
                    copy.start()
    for s in range(stages):
        for c in range(len(plans)):
            for copy in copies_of(c, s):
                copy.wait_send()
    base = (lax.axis_index("amp") * lax.axis_size("own") + lax.axis_index("own")) * fin_ref.shape[1]
    expand(base, fin_ref, lab_ref, rank_ref, out_ref)


def expand(base, x_ref, lab_ref, rank_ref, out_ref):
    share = x_ref.shape[1]
    count = lab_ref.shape[0]
    first = base // TILE
    row = base + lax.broadcasted_iota(jnp.int32, (share, LANES), 0)
    low = lax.broadcasted_iota(jnp.int32, (share, LANES), 1) < TILE
    row_lab = jnp.where(row < (first + 1) * TILE, lab_ref[first], lab_ref[jnp.minimum(first + 1, count - 1)])
    for u in range(0, count, 2):
        ranks = [rank_ref[u + h] for h in range(2)]
        turned = [pltpu.roll(x_ref[jnp.minimum(rank // 2, x_ref.shape[0] - 1)], (rank + h) % 2 * TILE, 1) for h, rank in enumerate(ranks)]
        match = row_lab == jnp.where(low, lab_ref[u], lab_ref[u + 1])
        out_ref[:, u * TILE : (u + 2) * TILE] = jnp.where(match, jnp.where(low, *turned), 0.0).astype(out_ref.dtype)


def shards(amplitudes, integrals, occ_irrep, tile_irrep):
    n_amp = lax.axis_size("amp")
    n_own = lax.axis_size("own")
    k_local, rows, width = amplitudes.shape
    n_tiles = tile_irrep.shape[0]
    slots = width * n_amp // TILE
    grain = gcd(width, TILE)
    chunks = NI * slots * TILE // LANES
    vmem, smem, hbm = (pl.BlockSpec(memory_space=m) for m in (pltpu.VMEM, pltpu.SMEM, pltpu.HBM))
    packed = pl.pallas_call(
        functools.partial(local_kernel, n_tiles, slots),
        out_shape=jax.ShapeDtypeStruct((chunks, rows, LANES), jnp.float32),
        in_specs=[hbm] * 4,
        out_specs=vmem,
        scratch_shapes=[
            pltpu.VMEM((k_local, width, rows), jnp.bfloat16),
            pltpu.VMEM((LABELS, k_local, width // grain, grain, rows), jnp.bfloat16),
            pltpu.SMEM(occ_irrep.shape, jnp.int32),
            pltpu.SMEM(tile_irrep.shape, jnp.int32),
            pltpu.SMEM((LABELS * slots,), jnp.int32),
            pltpu.SMEM((LABELS * NI * slots,), jnp.int32),
            pltpu.SMEM((LABELS,), jnp.int32),
            pltpu.SemaphoreType.DMA((3,)),
            pltpu.SemaphoreType.DMA((LABELS, width // grain)),
        ],
        compiler_params=pltpu.CompilerParams(vmem_limit_bytes=40 * 2**20),
        name="local",
    )(jnp.swapaxes(amplitudes, 1, 2), integrals, occ_irrep, tile_irrep)

    amp_bits, own_bits = n_amp.bit_length() - 1, n_own.bit_length() - 1
    share = rows // (n_amp * n_own)
    plans, scratch = [], []
    for order in orders(amp_bits, own_bits):
        left = [("amp", b) for b in reversed(range(amp_bits))] + [("own", b) for b in reversed(range(own_bits))]
        plan = []
        for name, bit in order:
            axis = left.index((name, bit))
            left.pop(axis)
            plan.append((name, bit, axis))
            lead = (2,) * len(left)
            whole = pltpu.VMEM(lead + (share, LANES), jnp.float32)
            coded = pltpu.VMEM(lead + (share, LANES), jnp.int16)
            scale = pltpu.VMEM(lead + (1, LANES), jnp.float32)
            scratch += [whole, whole] if not plan[1:] else [whole, coded, coded, scale, scale]
        plans.append(plan)
    stages = amp_bits + own_bits
    return pl.pallas_call(
        functools.partial(scatter_kernel, plans),
        out_shape=jax.ShapeDtypeStruct((share, rows), jnp.bfloat16),
        in_specs=[vmem, smem, smem],
        out_specs=vmem,
        scratch_shapes=scratch
        + [pltpu.VMEM((chunks, share, LANES), jnp.float32)]
        + [pltpu.SMEM((NI * n_tiles,), jnp.int32)] * 2
        + [pltpu.SemaphoreType.DMA((chunks, stages))] * 4,
        compiler_params=pltpu.CompilerParams(
            collective_id=0, has_side_effects=True, vmem_limit_bytes=40 * 2**20
        ),
        name="scatter",
    )(packed.reshape((chunks,) + (2,) * stages + (share, LANES)), occ_irrep, tile_irrep)


def solution(mesh):
    return jax.shard_map(
        shards,
        mesh=mesh,
        in_specs=(P("own", None, "amp"), P("own", None, None), P(), P()),
        out_specs=P(("amp", "own"), None),
        check_vma=False,
    )
```

```python
import functools
import itertools

import jax
import jax.numpy as jnp
from jax import lax
from jax.experimental import pallas as pl
from jax.experimental.pallas import tpu as pltpu
from jax.sharding import PartitionSpec as P

TILE = 64
NI = 2
LABELS = 8
LANES = 128
LEVELS = 32767.0
LEAST = 1e-30
MESH = pl.DeviceIdType.MESH


def gcd(a, b):
    return a if b == 0 else gcd(b, a % b)


def local_kernel(n_tiles, slots, amp_hbm, int_ref, occ_hbm, tile_hbm, out_ref, amp_ref, w_ref, occ_ref, tile_ref, tile_of, row_of, count, local_sems, sems):
    k_local, width, rows = amp_hbm.shape
    pieces, grain = w_ref.shape[2], w_ref.shape[3]
    wide = NI * slots
    amp_index = lax.axis_index("amp")
    own_index = lax.axis_index("own")

    amp_copy = pltpu.make_async_copy(amp_hbm, amp_ref, local_sems.at[0])
    occ_copy = pltpu.make_async_copy(occ_hbm, occ_ref, local_sems.at[1])
    tile_copy = pltpu.make_async_copy(tile_hbm, tile_ref, local_sems.at[2])
    tile_copy.start()
    occ_copy.start()
    amp_copy.start()

    for i in range(LABELS):
        count[i] = 0
        for s in range(slots):
            tile_of[i * slots + s] = -1
        for q in range(wide):
            row_of[i * wide + q] = -1
    tile_copy.wait()
    for t in range(n_tiles):
        lab = tile_ref[t]
        rank = count[lab]
        tile_of[lab * slots + rank] = t
        count[lab] = rank + 1

    def copy_of(lab, j):
        at = amp_index * width + j * grain
        t = tile_of[lab * slots + at // TILE]
        start = pl.multiple_of(jnp.maximum(t, 0) * TILE + at % TILE, grain)
        copy = pltpu.make_async_copy(int_ref.at[:, pl.ds(start, grain), :], w_ref.at[lab, :, j], sems.at[lab, j])
        return t, copy

    for lab in range(LABELS):
        for j in range(pieces):
            t, copy = copy_of(lab, j)

            @pl.when(t >= 0)
            def _():
                copy.start()

            @pl.when(t < 0)
            def _():
                w_ref[lab, :, j] = jnp.zeros((k_local, grain, rows), w_ref.dtype)

    for i in range(LABELS):
        count[i] = 0
    occ_copy.wait()
    for u in range(NI * n_tiles):
        lab = jnp.bitwise_xor(occ_ref[u // n_tiles], tile_ref[u % n_tiles])
        rank = count[lab]
        row_of[lab * wide + rank] = u
        count[lab] = rank + 1

    k_lab = [occ_ref[NI + own_index * k_local + k] for k in range(k_local)]

    amp_copy.wait()
    for lab in range(LABELS):
        for j in range(pieces):
            t, copy = copy_of(lab, j)

            @pl.when(t >= 0)
            def _():
                copy.wait()

    low = lax.broadcasted_iota(jnp.int32, (width, LANES), 1) < TILE

    def block(lab, carry):
        tiles = [jnp.maximum(row_of[lab * wide + q], 0) for q in range(wide)]
        lanes = [pl.ds(pl.multiple_of(u // 2 * LANES, LANES), LANES) for u in tiles]

        def gather(load):
            turned = [pltpu.roll(load(at), (u + q) % 2 * TILE, 1) for q, (at, u) in enumerate(zip(lanes, tiles))]
            return jnp.concatenate([jnp.where(low, *turned[q : q + 2]) for q in range(0, wide, 2)], axis=1)

        a = [gather(lambda at: amp_ref[k, :, at]) for k in range(k_local)]
        w = [
            gather(lambda at: w_ref[jnp.bitwise_xor(lab, k_lab[k]), k, :, :, at].reshape(width, LANES))
            for k in range(k_local)
        ]
        s = lax.dot_general(
            jnp.concatenate(a + w, axis=0),
            jnp.concatenate(w + a, axis=0),
            (((0,), (0,)), ((), ())),
            preferred_element_type=jnp.float32,
        )
        for q in range(wide):
            u = row_of[lab * wide + q]

            @pl.when(u >= 0)
            def _():
                for c in range(out_ref.shape[0]):
                    out_ref[c, pl.ds(pl.multiple_of(u * TILE, TILE), TILE), :] = s[
                        q * TILE : (q + 1) * TILE, c * LANES : (c + 1) * LANES
                    ]

        return carry

    lax.fori_loop(0, LABELS, block, 0)


def orders(amp_bits, own_bits):
    core = [("amp", 0)]
    y = [("amp", b) for b in range(1, amp_bits)]
    near = [("own", 0)]
    far = [("own", b) for b in range(1, own_bits)]
    return [core + y + near + far, core + near + y + far, core + far + y + near]


def bit_of(name, bit):
    return lax.axis_index(name) // 2**bit % 2


def partner_of(name, bit):
    return {name: lax.axis_index(name) + (1 - 2 * bit_of(name, bit)) * 2**bit}


def scatter_kernel(plans, x_ref, occ_ref, tile_ref, out_ref, *scratch):
    stages = len(plans[0])
    bufs, at = [], 0
    for c in range(len(plans)):
        bufs.append([])
        for s in range(stages):
            take = 2 if s == 0 else 5
            bufs[c].append(scratch[at : at + take])
            at += take
    fin_ref, lab_ref, rank_ref, send_sems, recv_sems, scale_send_sems, scale_recv_sems = scratch[at:]

    barrier = pltpu.get_barrier_semaphore()
    for name, bit, _ in plans[0]:
        pl.semaphore_signal(barrier, inc=1, device_id=partner_of(name, bit), device_id_type=MESH)
    pl.semaphore_wait(barrier, stages)

    def remote(c, s, src, dst, send, recv):
        name, bit, _ = plans[c][s]
        return pltpu.make_async_remote_copy(
            src_ref=src,
            dst_ref=dst,
            send_sem=send.at[c, s],
            recv_sem=recv.at[c, s],
            device_id=partner_of(name, bit),
            device_id_type=MESH,
        )

    def copies_of(c, s):
        name, bit, axis = plans[c][s]
        if s == 0:
            src = x_ref.at[(c,) + (slice(None),) * axis + (1 - bit_of(name, bit),)]
            return [remote(c, s, src, bufs[c][s][1], send_sems, recv_sems)]
        _, q_send, q_recv, scale_send, scale_recv = bufs[c][s]
        return [
            remote(c, s, scale_send, scale_recv, scale_send_sems, scale_recv_sems),
            remote(c, s, q_send, q_recv, send_sems, recv_sems),
        ]

    def blocks(count):
        return itertools.product(range(2), repeat=count)

    def total_of(c, s, index):
        name, bit, axis = plans[c][s]
        kept = index[:axis] + (bit_of(name, bit),) + index[axis:]
        if s == 0:
            return x_ref[(c,) + kept] + bufs[c][s][1][index]
        _, _, q_recv, _, scale_recv = bufs[c][s]
        return bufs[c][s - 1][0][kept] + q_recv[index].astype(jnp.int32).astype(jnp.float32) * scale_recv[index]

    def quantize(c, s):
        name, bit, axis = plans[c][s]
        _, q_send, _, scale_send, _ = bufs[c][s]
        away = 1 - bit_of(name, bit)
        for index in blocks(stages - 1 - s):
            x = total_of(c, s - 1, index[:axis] + (away,) + index[axis:])
            most = jnp.maximum(jnp.max(jnp.abs(x), axis=0, keepdims=True), LEAST)
            q_send[index] = jnp.round(x * (LEVELS / most)).astype(jnp.int32).astype(jnp.int16)
            scale_send[index] = most * (1.0 / LEVELS)

    for c in range(len(plans)):
        for copy in copies_of(c, 0):
            copy.start()
    n_tiles = tile_ref.shape[0]
    labs = [jnp.bitwise_xor(occ_ref[u // n_tiles], tile_ref[u % n_tiles]) for u in range(NI * n_tiles)]
    for u, lab in enumerate(labs):
        lab_ref[u] = lab
        rank = jnp.int32(0)
        for other in labs[:u]:
            rank = rank + jnp.where(other == lab, 1, 0)
        rank_ref[u] = rank
    for s in range(stages):
        for c in range(len(plans)):
            for copy in copies_of(c, s):
                copy.wait_recv()
            if s + 1 == stages:
                fin_ref[c] = total_of(c, s, ())
                continue
            quantize(c, s + 1)
            for copy in copies_of(c, s + 1):
                copy.start()
            name, bit, axis = plans[c][s + 1]
            for index in blocks(stages - 2 - s):
                kept = index[:axis] + (bit_of(name, bit),) + index[axis:]
                bufs[c][s][0][kept] = total_of(c, s, kept)
    for s in range(stages):
        for c in range(len(plans)):
            for copy in copies_of(c, s):
                copy.wait_send()
    base = (lax.axis_index("amp") * lax.axis_size("own") + lax.axis_index("own")) * fin_ref.shape[1]
    expand(base, fin_ref, lab_ref, rank_ref, out_ref)


def expand(base, x_ref, lab_ref, rank_ref, out_ref):
    share = x_ref.shape[1]
    count = lab_ref.shape[0]
    first = base // TILE
    row = base + lax.broadcasted_iota(jnp.int32, (share, LANES), 0)
    low = lax.broadcasted_iota(jnp.int32, (share, LANES), 1) < TILE
    row_lab = jnp.where(row < (first + 1) * TILE, lab_ref[first], lab_ref[jnp.minimum(first + 1, count - 1)])
    for u in range(0, count, 2):
        ranks = [rank_ref[u + h] for h in range(2)]
        turned = [pltpu.roll(x_ref[jnp.minimum(rank // 2, x_ref.shape[0] - 1)], (rank + h) % 2 * TILE, 1) for h, rank in enumerate(ranks)]
        match = row_lab == jnp.where(low, lab_ref[u], lab_ref[u + 1])
        out_ref[:, u * TILE : (u + 2) * TILE] = jnp.where(match, jnp.where(low, *turned), 0.0).astype(out_ref.dtype)


def shards(amplitudes, integrals, occ_irrep, tile_irrep):
    n_amp = lax.axis_size("amp")
    n_own = lax.axis_size("own")
    k_local, rows, width = amplitudes.shape
    n_tiles = tile_irrep.shape[0]
    slots = width * n_amp // TILE
    grain = gcd(width, TILE)
    chunks = NI * slots * TILE // LANES
    vmem, smem, hbm = (pl.BlockSpec(memory_space=m) for m in (pltpu.VMEM, pltpu.SMEM, pltpu.HBM))
    packed = pl.pallas_call(
        functools.partial(local_kernel, n_tiles, slots),
        out_shape=jax.ShapeDtypeStruct((chunks, rows, LANES), jnp.float32),
        in_specs=[hbm] * 4,
        out_specs=vmem,
        scratch_shapes=[
            pltpu.VMEM((k_local, width, rows), jnp.bfloat16),
            pltpu.VMEM((LABELS, k_local, width // grain, grain, rows), jnp.bfloat16),
            pltpu.SMEM(occ_irrep.shape, jnp.int32),
            pltpu.SMEM(tile_irrep.shape, jnp.int32),
            pltpu.SMEM((LABELS * slots,), jnp.int32),
            pltpu.SMEM((LABELS * NI * slots,), jnp.int32),
            pltpu.SMEM((LABELS,), jnp.int32),
            pltpu.SemaphoreType.DMA((3,)),
            pltpu.SemaphoreType.DMA((LABELS, width // grain)),
        ],
        compiler_params=pltpu.CompilerParams(vmem_limit_bytes=40 * 2**20),
        name="local",
    )(jnp.swapaxes(amplitudes, 1, 2), integrals, occ_irrep, tile_irrep)

    amp_bits, own_bits = n_amp.bit_length() - 1, n_own.bit_length() - 1
    share = rows // (n_amp * n_own)
    plans, scratch = [], []
    for order in orders(amp_bits, own_bits):
        left = [("amp", b) for b in reversed(range(amp_bits))] + [("own", b) for b in reversed(range(own_bits))]
        plan = []
        for name, bit in order:
            axis = left.index((name, bit))
            left.pop(axis)
            plan.append((name, bit, axis))
            lead = (2,) * len(left)
            whole = pltpu.VMEM(lead + (share, LANES), jnp.float32)
            coded = pltpu.VMEM(lead + (share, LANES), jnp.int16)
            scale = pltpu.VMEM(lead + (1, LANES), jnp.float32)
            scratch += [whole, whole] if not plan[1:] else [whole, coded, coded, scale, scale]
        plans.append(plan)
    stages = amp_bits + own_bits
    return pl.pallas_call(
        functools.partial(scatter_kernel, plans),
        out_shape=jax.ShapeDtypeStruct((share, rows), jnp.bfloat16),
        in_specs=[vmem, smem, smem],
        out_specs=vmem,
        scratch_shapes=scratch
        + [pltpu.VMEM((chunks, share, LANES), jnp.float32)]
        + [pltpu.SMEM((NI * n_tiles,), jnp.int32)] * 2
        + [pltpu.SemaphoreType.DMA((chunks, stages))] * 4,
        compiler_params=pltpu.CompilerParams(
            collective_id=0, has_side_effects=True, vmem_limit_bytes=40 * 2**20
        ),
        name="scatter",
    )(packed.reshape((chunks,) + (2,) * stages + (share, LANES)), occ_irrep, tile_irrep)


def solution(mesh):
    return jax.shard_map(
        shards,
        mesh=mesh,
        in_specs=(P("own", None, "amp"), P("own", None, None), P(), P()),
        out_specs=P(("amp", "own"), None),
        check_vma=False,
    )
```

```python
import functools
import itertools

import jax
import jax.numpy as jnp
from jax import lax
from jax.experimental import pallas as pl
from jax.experimental.pallas import tpu as pltpu
from jax.sharding import PartitionSpec as P

TILE = 64
NI = 2
LABELS = 8
LANES = 128
LEVELS = 32767.0
LEAST = 1e-30
MESH = pl.DeviceIdType.MESH


def gcd(a, b):
    return a if b == 0 else gcd(b, a % b)


def local_kernel(n_tiles, slots, amp_ref, int_ref, occ_hbm, tile_hbm, out_ref, w_ref, occ_ref, tile_ref, tile_of, row_of, count, local_sems, sems):
    k_local, width, rows = amp_ref.shape
    pieces, grain = w_ref.shape[2], w_ref.shape[3]
    wide = NI * slots
    amp_index = lax.axis_index("amp")
    own_index = lax.axis_index("own")

    occ_copy = pltpu.make_async_copy(occ_hbm, occ_ref, local_sems.at[1])
    tile_copy = pltpu.make_async_copy(tile_hbm, tile_ref, local_sems.at[2])
    tile_copy.start()
    occ_copy.start()

    for i in range(LABELS):
        count[i] = 0
        for s in range(slots):
            tile_of[i * slots + s] = -1
        for q in range(wide):
            row_of[i * wide + q] = -1
    tile_copy.wait()
    for t in range(n_tiles):
        lab = tile_ref[t]
        rank = count[lab]
        tile_of[lab * slots + rank] = t
        count[lab] = rank + 1

    def copy_of(lab, j):
        at = amp_index * width + j * grain
        t = tile_of[lab * slots + at // TILE]
        start = pl.multiple_of(jnp.maximum(t, 0) * TILE + at % TILE, grain)
        copy = pltpu.make_async_copy(int_ref.at[:, pl.ds(start, grain), :], w_ref.at[lab, :, j], sems.at[lab, j])
        return t, copy

    for lab in range(LABELS):
        for j in range(pieces):
            t, copy = copy_of(lab, j)

            @pl.when(t >= 0)
            def _():
                copy.start()

            @pl.when(t < 0)
            def _():
                w_ref[lab, :, j] = jnp.zeros((k_local, grain, rows), w_ref.dtype)

    for i in range(LABELS):
        count[i] = 0
    occ_copy.wait()
    for u in range(NI * n_tiles):
        lab = jnp.bitwise_xor(occ_ref[u // n_tiles], tile_ref[u % n_tiles])
        rank = count[lab]
        row_of[lab * wide + rank] = u
        count[lab] = rank + 1

    k_lab = [occ_ref[NI + own_index * k_local + k] for k in range(k_local)]

    for lab in range(LABELS):
        for j in range(pieces):
            t, copy = copy_of(lab, j)

            @pl.when(t >= 0)
            def _():
                copy.wait()

    low = lax.broadcasted_iota(jnp.int32, (width, LANES), 1) < TILE

    def block(lab, carry):
        tiles = [jnp.maximum(row_of[lab * wide + q], 0) for q in range(wide)]
        lanes = [pl.ds(pl.multiple_of(u // 2 * LANES, LANES), LANES) for u in tiles]

        def gather(load):
            turned = [pltpu.roll(load(at), (u + q) % 2 * TILE, 1) for q, (at, u) in enumerate(zip(lanes, tiles))]
            return jnp.concatenate([jnp.where(low, *turned[q : q + 2]) for q in range(0, wide, 2)], axis=1)

        a = [gather(lambda at: amp_ref[k, :, at]) for k in range(k_local)]
        w = [
            gather(lambda at: w_ref[jnp.bitwise_xor(lab, k_lab[k]), k, :, :, at].reshape(width, LANES))
            for k in range(k_local)
        ]
        s = lax.dot_general(
            jnp.concatenate(a + w, axis=0),
            jnp.concatenate(w + a, axis=0),
            (((0,), (0,)), ((), ())),
            preferred_element_type=jnp.float32,
        )
        for q in range(wide):
            u = row_of[lab * wide + q]

            @pl.when(u >= 0)
            def _():
                for c in range(out_ref.shape[0]):
                    out_ref[c, pl.ds(pl.multiple_of(u * TILE, TILE), TILE), :] = s[
                        q * TILE : (q + 1) * TILE, c * LANES : (c + 1) * LANES
                    ]

        return carry

    lax.fori_loop(0, LABELS, block, 0)


def orders(amp_bits, own_bits):
    core = [("amp", 0)]
    y = [("amp", b) for b in range(1, amp_bits)]
    near = [("own", 0)]
    far = [("own", b) for b in range(1, own_bits)]
    return [core + y + near + far, core + near + y + far, core + far + y + near]


def bit_of(name, bit):
    return lax.axis_index(name) // 2**bit % 2


def partner_of(name, bit):
    return {name: lax.axis_index(name) + (1 - 2 * bit_of(name, bit)) * 2**bit}


def scatter_kernel(plans, x_ref, occ_ref, tile_ref, out_ref, *scratch):
    stages = len(plans[0])
    bufs, at = [], 0
    for c in range(len(plans)):
        bufs.append([])
        for s in range(stages):
            take = 2 if s == 0 else 5
            bufs[c].append(scratch[at : at + take])
            at += take
    fin_ref, lab_ref, rank_ref, send_sems, recv_sems, scale_send_sems, scale_recv_sems = scratch[at:]

    barrier = pltpu.get_barrier_semaphore()
    for name, bit, _ in plans[0]:
        pl.semaphore_signal(barrier, inc=1, device_id=partner_of(name, bit), device_id_type=MESH)
    pl.semaphore_wait(barrier, stages)

    def remote(c, s, src, dst, send, recv):
        name, bit, _ = plans[c][s]
        return pltpu.make_async_remote_copy(
            src_ref=src,
            dst_ref=dst,
            send_sem=send.at[c, s],
            recv_sem=recv.at[c, s],
            device_id=partner_of(name, bit),
            device_id_type=MESH,
        )

    def copies_of(c, s):
        name, bit, axis = plans[c][s]
        if s == 0:
            src = x_ref.at[(c,) + (slice(None),) * axis + (1 - bit_of(name, bit),)]
            return [remote(c, s, src, bufs[c][s][1], send_sems, recv_sems)]
        _, q_send, q_recv, scale_send, scale_recv = bufs[c][s]
        return [
            remote(c, s, scale_send, scale_recv, scale_send_sems, scale_recv_sems),
            remote(c, s, q_send, q_recv, send_sems, recv_sems),
        ]

    def blocks(count):
        return itertools.product(range(2), repeat=count)

    def total_of(c, s, index):
        name, bit, axis = plans[c][s]
        kept = index[:axis] + (bit_of(name, bit),) + index[axis:]
        if s == 0:
            return x_ref[(c,) + kept] + bufs[c][s][1][index]
        _, _, q_recv, _, scale_recv = bufs[c][s]
        return bufs[c][s - 1][0][kept] + q_recv[index].astype(jnp.int32).astype(jnp.float32) * scale_recv[index]

    def quantize(c, s):
        name, bit, axis = plans[c][s]
        _, q_send, _, scale_send, _ = bufs[c][s]
        away = 1 - bit_of(name, bit)
        for index in blocks(stages - 1 - s):
            x = total_of(c, s - 1, index[:axis] + (away,) + index[axis:])
            most = jnp.maximum(jnp.max(jnp.abs(x), axis=0, keepdims=True), LEAST)
            q_send[index] = jnp.round(x * (LEVELS / most)).astype(jnp.int32).astype(jnp.int16)
            scale_send[index] = most * (1.0 / LEVELS)

    for c in range(len(plans)):
        for copy in copies_of(c, 0):
            copy.start()
    n_tiles = tile_ref.shape[0]
    labs = [jnp.bitwise_xor(occ_ref[u // n_tiles], tile_ref[u % n_tiles]) for u in range(NI * n_tiles)]
    for u, lab in enumerate(labs):
        lab_ref[u] = lab
        rank = jnp.int32(0)
        for other in labs[:u]:
            rank = rank + jnp.where(other == lab, 1, 0)
        rank_ref[u] = rank
    for s in range(stages):
        for c in range(len(plans)):
            for copy in copies_of(c, s):
                copy.wait_recv()
            if s + 1 == stages:
                fin_ref[c] = total_of(c, s, ())
                continue
            quantize(c, s + 1)
            for copy in copies_of(c, s + 1):
                copy.start()
            name, bit, axis = plans[c][s + 1]
            for index in blocks(stages - 2 - s):
                kept = index[:axis] + (bit_of(name, bit),) + index[axis:]
                bufs[c][s][0][kept] = total_of(c, s, kept)
    for s in range(stages):
        for c in range(len(plans)):
            for copy in copies_of(c, s):
                copy.wait_send()
    base = (lax.axis_index("amp") * lax.axis_size("own") + lax.axis_index("own")) * fin_ref.shape[1]
    expand(base, fin_ref, lab_ref, rank_ref, out_ref)


def expand(base, x_ref, lab_ref, rank_ref, out_ref):
    share = x_ref.shape[1]
    count = lab_ref.shape[0]
    first = base // TILE
    row = base + lax.broadcasted_iota(jnp.int32, (share, LANES), 0)
    low = lax.broadcasted_iota(jnp.int32, (share, LANES), 1) < TILE
    row_lab = jnp.where(row < (first + 1) * TILE, lab_ref[first], lab_ref[jnp.minimum(first + 1, count - 1)])
    for u in range(0, count, 2):
        ranks = [rank_ref[u + h] for h in range(2)]
        turned = [pltpu.roll(x_ref[jnp.minimum(rank // 2, x_ref.shape[0] - 1)], (rank + h) % 2 * TILE, 1) for h, rank in enumerate(ranks)]
        match = row_lab == jnp.where(low, lab_ref[u], lab_ref[u + 1])
        out_ref[:, u * TILE : (u + 2) * TILE] = jnp.where(match, jnp.where(low, *turned), 0.0).astype(out_ref.dtype)


def shards(amplitudes, integrals, occ_irrep, tile_irrep):
    n_amp = lax.axis_size("amp")
    n_own = lax.axis_size("own")
    k_local, rows, width = amplitudes.shape
    n_tiles = tile_irrep.shape[0]
    slots = width * n_amp // TILE
    grain = gcd(width, TILE)
    chunks = NI * slots * TILE // LANES
    vmem, smem, hbm = (pl.BlockSpec(memory_space=m) for m in (pltpu.VMEM, pltpu.SMEM, pltpu.HBM))
    packed = pl.pallas_call(
        functools.partial(local_kernel, n_tiles, slots),
        out_shape=jax.ShapeDtypeStruct((chunks, rows, LANES), jnp.float32),
        in_specs=[vmem] + [hbm] * 3,
        out_specs=vmem,
        scratch_shapes=[
            pltpu.VMEM((LABELS, k_local, width // grain, grain, rows), jnp.bfloat16),
            pltpu.SMEM(occ_irrep.shape, jnp.int32),
            pltpu.SMEM(tile_irrep.shape, jnp.int32),
            pltpu.SMEM((LABELS * slots,), jnp.int32),
            pltpu.SMEM((LABELS * NI * slots,), jnp.int32),
            pltpu.SMEM((LABELS,), jnp.int32),
            pltpu.SemaphoreType.DMA((3,)),
            pltpu.SemaphoreType.DMA((LABELS, width // grain)),
        ],
        compiler_params=pltpu.CompilerParams(vmem_limit_bytes=40 * 2**20),
        name="local",
    )(jnp.swapaxes(amplitudes, 1, 2), integrals, occ_irrep, tile_irrep)

    amp_bits, own_bits = n_amp.bit_length() - 1, n_own.bit_length() - 1
    share = rows // (n_amp * n_own)
    plans, scratch = [], []
    for order in orders(amp_bits, own_bits):
        left = [("amp", b) for b in reversed(range(amp_bits))] + [("own", b) for b in reversed(range(own_bits))]
        plan = []
        for name, bit in order:
            axis = left.index((name, bit))
            left.pop(axis)
            plan.append((name, bit, axis))
            lead = (2,) * len(left)
            whole = pltpu.VMEM(lead + (share, LANES), jnp.float32)
            coded = pltpu.VMEM(lead + (share, LANES), jnp.int16)
            scale = pltpu.VMEM(lead + (1, LANES), jnp.float32)
            scratch += [whole, whole] if not plan[1:] else [whole, coded, coded, scale, scale]
        plans.append(plan)
    stages = amp_bits + own_bits
    return pl.pallas_call(
        functools.partial(scatter_kernel, plans),
        out_shape=jax.ShapeDtypeStruct((share, rows), jnp.bfloat16),
        in_specs=[vmem, smem, smem],
        out_specs=vmem,
        scratch_shapes=scratch
        + [pltpu.VMEM((chunks, share, LANES), jnp.float32)]
        + [pltpu.SMEM((NI * n_tiles,), jnp.int32)] * 2
        + [pltpu.SemaphoreType.DMA((chunks, stages))] * 4,
        compiler_params=pltpu.CompilerParams(
            collective_id=0, has_side_effects=True, vmem_limit_bytes=40 * 2**20
        ),
        name="scatter",
    )(packed.reshape((chunks,) + (2,) * stages + (share, LANES)), occ_irrep, tile_irrep)


def solution(mesh):
    return jax.shard_map(
        shards,
        mesh=mesh,
        in_specs=(P("own", None, "amp"), P("own", None, None), P(), P()),
        out_specs=P(("amp", "own"), None),
        check_vma=False,
    )
```
